32 devices in a mesh: seq: 2 (over core), ctx: 4 (over y, x), fsdp: 4 (over z).
Axes of the slice: x: 2, y: 2, z: 4, core: 2. Of those that a mesh axis runs over, the one named last changes fastest.
Arguments:
- tokens: bfloat16 [2, 2048, 576], P('seq', ('ctx', 'fsdp')), may hold values from -6 to 6
- block_order: int32 [2, 8], P('seq'), may hold values from 0 to 7, each once within a row
- attn_gain: bfloat16 [576], P('fsdp'), may hold values from 0.25 to 1.75
- mlp_gain: bfloat16 [576], P('fsdp'), may hold values from 0.25 to 1.75
- w_query: bfloat16 [576, 576], P('fsdp'), may hold values from -0.25 to 0.25
- w_key: bfloat16 [576, 192], P('fsdp'), may hold values from -0.25 to 0.25
- w_value: bfloat16 [576, 192], P('fsdp'), may hold values from -0.25 to 0.25
- w_out: bfloat16 [576, 576], P(None, 'fsdp'), may hold values from -6 to 6
- w_gate: bfloat16 [576, 1536], P('fsdp'), may hold values from -0.25 to 0.25
- w_up: bfloat16 [576, 1536], P('fsdp'), may hold values from -0.25 to 0.25
- w_down: bfloat16 [1536, 576], P(None, 'fsdp'), may hold values from -0.15625 to 0.15625
- cotangent: bfloat16 [2, 2048, 576], P('seq', ('ctx', 'fsdp')), may hold values from -6 to 6
Outputs:
- layer_out: bfloat16 [2, 2048, 576], P('seq', ('ctx', 'fsdp'))
- input_grad: bfloat16 [2, 2048, 576], P('seq', ('ctx', 'fsdp'))
- attn_gain_grad: float32 [576], P('fsdp')
- mlp_gain_grad: float32 [576], P('fsdp')
- w_query_grad: float32 [576, 576], P('fsdp')
- w_key_grad: float32 [576, 192], P('fsdp')
- w_value_grad: float32 [576, 192], P('fsdp')
- w_out_grad: float32 [576, 576], P(None, 'fsdp')
- w_gate_grad: float32 [576, 1536], P('fsdp')
- w_up_grad: float32 [576, 1536], P('fsdp')
- w_down_grad: float32 [1536, 576], P(None, 'fsdp')
The draws below stay inside these ranges and needn't reach their ends.
Inputs may be any that keep to these rules, and one draw needn't show every extreme that they name: Each row of block_order names every place 0 to 7 once.
All inputs are finite; a program needn't handle non-finite values.
Results may differ from the reference program's by a relative error of at most 0.015.
Values may be sent and summed in bfloat16 or wider, within the bound.
No kernel may reach another device: no remote copies, remote signals or barrier semaphores. Data moves between devices by JAX's collectives and lax.ppermute only.
A program may use at most 192 MiB of HBM per device.

```python
import math
import jax
import jax.numpy as jnp
from jax import lax

D = 576
H = 9
KVH = 3
HD = 64
FF = 1536
SEQS = 2
SEQLEN = 2048
NBLK = 8
BLK = 256


def shard_levels(rng, shape, split, low, largest):
    def one(position, shards_of):
        heights = jax.random.uniform(jax.random.fold_in(jax.random.fold_in(rng, 6), position), (shards_of,), jnp.float32, low / len(split), largest / len(split))
        return jnp.repeat(jnp.exp(heights), shape[position] // shards_of).reshape((-1,) + (1,) * (len(shape) - position - 1))

    level = one(*split[0])
    for cut in split[1:]:
        level = level * one(*cut)
    return level


def centred(own_key, extent, width, limit, shards=(), kind=jnp.bfloat16):
    level = shard_levels(own_key, extent, shards, -0.22, 0.18) if shards else 1.0
    array = jax.random.normal(own_key, extent, jnp.float32) * width * level
    return jnp.minimum(jnp.maximum(array, -limit), limit).astype(kind)


def setup_inputs(seed: int = 0) -> dict:
    seeds = jax.random.split(jax.random.key(seed), 13)
    tokens = centred(seeds[0], (SEQS, SEQLEN, D), 1.0, 6.0, ((0, 2), (1, 16)))
    block_order = jax.vmap(lambda own: jax.random.permutation(own, NBLK))(jax.random.split(seeds[1], SEQS)).reshape((SEQS, NBLK)).astype(jnp.int32)
    attn_gain = jnp.clip(1.0 + 0.15 * jax.random.normal(seeds[2], (D,), jnp.float32), 0.25, 1.75).astype(jnp.bfloat16)
    mlp_gain = jnp.clip(1.0 + 0.15 * jax.random.normal(seeds[3], (D,), jnp.float32), 0.25, 1.75).astype(jnp.bfloat16)
    w_query = centred(seeds[4], (D, H * HD), D ** -0.5, 0.25, ((0, 4),))
    w_key = centred(seeds[5], (D, KVH * HD), D ** -0.5, 0.25, ((0, 4),))
    w_value = centred(seeds[6], (D, KVH * HD), D ** -0.5, 0.25, ((0, 4),))
    w_out = centred(seeds[7], (H * HD, D), 1 ** -0.5, 6.0, ((1, 4),))
    w_gate = centred(seeds[8], (D, FF), D ** -0.5, 0.25, ((0, 4),))
    w_up = centred(seeds[9], (D, FF), D ** -0.5, 0.25, ((0, 4),))
    w_down = centred(seeds[10], (FF, D), FF ** -0.5, 0.15625, ((1, 4),))
    cotangent = centred(seeds[11], (SEQS, SEQLEN, D), 1.0, 6.0, ((0, 2), (1, 16)))
    return {"tokens": tokens, "block_order": block_order, "attn_gain": attn_gain, "mlp_gain": mlp_gain, "w_query": w_query, "w_key": w_key, "w_value": w_value, "w_out": w_out, "w_gate": w_gate, "w_up": w_up, "w_down": w_down, "cotangent": cotangent}


EPS = 1e-05
THETA = 100000.0
NEGATIVE = -1e+30

def rms_scale(rows):
    return lax.rsqrt(lax.optimization_barrier(jnp.mean(rows * rows, axis=-1, keepdims=True)) + EPS)

def rotary_tables(positions):
    half = HD // 2
    inverse = jnp.power(THETA, -jnp.arange(half, dtype=jnp.float32) * 2.0 / HD)
    angles = positions.astype(jnp.float32)[:, None] * inverse[None, :]
    angles = jnp.concatenate([angles, angles], axis=1)
    return (jnp.cos(angles)[:, None, :], jnp.sin(angles)[:, None, :])

def rotate(values, cosines, sines):
    half = HD // 2
    turned = jnp.concatenate([-values[..., half:], values[..., :half]], axis=-1)
    return values * cosines + turned * sines

def attend_forward(queries, keys, values, query_block):
    count = SEQLEN // query_block
    group = H // KVH
    score_scale = HD ** (-0.5)

    def one_block(item):
        index, block_q = item
        rows = index * query_block + jnp.arange(query_block, dtype=jnp.int32)

        def step(key_index, state):
            top, total, accumulated = state
            start = key_index * query_block
            block_k = lax.dynamic_slice_in_dim(keys, start, query_block, 0)
            block_v = lax.dynamic_slice_in_dim(values, start, query_block, 0)
            columns = start + jnp.arange(query_block, dtype=jnp.int32)
            scores = jnp.einsum('qcgd,kcd->cgqk', block_q.astype(jnp.float32), block_k.astype(jnp.float32)) * score_scale
            allowed = rows[:, None] >= columns[None, :]
            masked = jnp.where(allowed, scores, NEGATIVE)
            new_top = jnp.maximum(top, lax.optimization_barrier(jnp.max(masked, axis=-1)))
            weights = jnp.where(allowed, jnp.exp(masked - new_top[..., None]), 0.0)
            factor = jnp.exp(top - new_top)
            total = factor * total + lax.optimization_barrier(jnp.sum(weights, axis=-1))
            rounded = lax.optimization_barrier(weights.astype(jnp.bfloat16)).astype(jnp.float32)
            accumulated = factor[..., None] * accumulated + jnp.einsum('cgqk,kcd->cgqd', rounded, block_v.astype(jnp.float32))
            return (new_top, total, accumulated)
        start_state = (jnp.full((KVH, group, query_block), NEGATIVE, jnp.float32), jnp.zeros((KVH, group, query_block), jnp.float32), jnp.zeros((KVH, group, query_block, HD), jnp.float32))
        top, total, accumulated = lax.fori_loop(0, index + 1, step, start_state)
        attended = (accumulated / total[..., None]).transpose(2, 0, 1, 3).reshape(query_block, H * HD)
        return (attended.astype(jnp.bfloat16), top + jnp.log(total))
    blocks_q = queries.reshape(count, query_block, KVH, group, HD)
    attended, log_total = lax.map(one_block, (jnp.arange(count, dtype=jnp.int32), blocks_q))
    return (attended.reshape(SEQLEN, H * HD), log_total)

def attend_backward(queries, keys, values, attended, attended_grad, log_total, query_block):
    count = SEQLEN // query_block
    group = H // KVH
    score_scale = HD ** (-0.5)
    grad_heads = attended_grad.reshape(SEQLEN, KVH, group, HD)
    delta = lax.optimization_barrier(jnp.sum(grad_heads.astype(jnp.float32) * attended.reshape(SEQLEN, KVH, group, HD).astype(jnp.float32), axis=-1))
    blocks_q = queries.reshape(count, query_block, KVH, group, HD)
    blocks_g = grad_heads.reshape(count, query_block, KVH, group, HD)
    blocks_d = delta.reshape(count, query_block, KVH, group).transpose(0, 2, 3, 1)

    def one_block(carry, item):
        index, block_q, block_g, block_l, block_d = item
        rows = index * query_block + jnp.arange(query_block, dtype=jnp.int32)

        def step(key_index, state):
            query_grad, key_grad, value_grad = state
            start = key_index * query_block
            block_k = lax.dynamic_slice_in_dim(keys, start, query_block, 0).astype(jnp.float32)
            block_v = lax.dynamic_slice_in_dim(values, start, query_block, 0).astype(jnp.float32)
            columns = start + jnp.arange(query_block, dtype=jnp.int32)
            scores = jnp.einsum('qcgd,kcd->cgqk', block_q.astype(jnp.float32), block_k) * score_scale
            allowed = rows[:, None] >= columns[None, :]
            masked = jnp.where(allowed, scores, NEGATIVE)
            probabilities = jnp.where(allowed, jnp.exp(masked - block_l[..., None]), 0.0)
            rounded = lax.optimization_barrier(probabilities.astype(jnp.bfloat16)).astype(jnp.float32)
            value_part = jnp.einsum('cgqk,qcgd->kcd', rounded, block_g.astype(jnp.float32))
            value_grad = lax.dynamic_update_slice_in_dim(value_grad, lax.dynamic_slice_in_dim(value_grad, start, query_block, 0) + value_part, start, 0)
            prob_grad = jnp.einsum('qcgd,kcd->cgqk', block_g.astype(jnp.float32), block_v)
            score_grad = lax.optimization_barrier((probabilities * (prob_grad - block_d[..., None])).astype(jnp.bfloat16)).astype(jnp.float32)
            query_grad = query_grad + jnp.einsum('cgqk,kcd->qcgd', score_grad, block_k)
            key_part = jnp.einsum('cgqk,qcgd->kcd', score_grad, block_q.astype(jnp.float32))
            key_grad = lax.dynamic_update_slice_in_dim(key_grad, lax.dynamic_slice_in_dim(key_grad, start, query_block, 0) + key_part, start, 0)
            return (query_grad, key_grad, value_grad)
        key_grad, value_grad = carry
        start_grad = jnp.zeros((query_block, KVH, group, HD), jnp.float32)
        query_grad, key_grad, value_grad = lax.fori_loop(0, index + 1, step, (start_grad, key_grad, value_grad))
        return ((key_grad, value_grad), query_grad)
    zeros = jnp.zeros((SEQLEN, KVH, HD), jnp.float32)
    (key_grad, value_grad), query_grad = lax.scan(one_block, (zeros, zeros), (jnp.arange(count, dtype=jnp.int32), blocks_q, blocks_g, log_total, blocks_d))
    query_grad = query_grad.reshape(SEQLEN, KVH, group, HD) * score_scale
    return (query_grad, key_grad * score_scale, value_grad)

def outer_sum(left, right):
    return jnp.dot(left.T, right, preferred_element_type=jnp.float32)

def reference(tokens, block_order, attn_gain, mlp_gain, w_query, w_key, w_value, w_out, w_gate, w_up, w_down, cotangent):
    group = H // KVH
    query_block = math.gcd(SEQLEN, 512)
    gain_one = attn_gain.astype(jnp.float32)
    gain_two = mlp_gain.astype(jnp.float32)
    natural = jnp.arange(SEQLEN, dtype=jnp.int32)
    cosines, sines = rotary_tables(natural)
    outputs = []
    input_grads = []
    totals = None
    for sequence in range(SEQS):
        positions = (block_order[sequence][natural // BLK] * BLK + natural % BLK).astype(jnp.int32)
        inputs = jnp.zeros((SEQLEN, D), jnp.float32).at[positions].set(tokens[sequence].astype(jnp.float32))
        grad_out = jnp.zeros((SEQLEN, D), jnp.bfloat16).at[positions].set(cotangent[sequence])
        scale_one = rms_scale(inputs)
        normed_one = inputs * scale_one
        hidden_one = (normed_one * gain_one).astype(jnp.bfloat16)
        queries = rotate(jnp.dot(hidden_one, w_query, preferred_element_type=jnp.float32).reshape(SEQLEN, H, HD), cosines, sines)
        queries = queries.astype(jnp.bfloat16).reshape(SEQLEN, KVH, group, HD)
        keys = rotate(jnp.dot(hidden_one, w_key, preferred_element_type=jnp.float32).reshape(SEQLEN, KVH, HD), cosines, sines).astype(jnp.bfloat16)
        values = jnp.dot(hidden_one, w_value, preferred_element_type=jnp.float32).astype(jnp.bfloat16)
        attended, log_total = attend_forward(queries, keys, values.reshape(SEQLEN, KVH, HD), query_block)
        mid = inputs + jnp.dot(attended, w_out, preferred_element_type=jnp.float32)
        scale_two = rms_scale(mid)
        normed_two = mid * scale_two
        hidden_two = (normed_two * gain_two).astype(jnp.bfloat16)
        gate = jnp.dot(hidden_two, w_gate, preferred_element_type=jnp.float32)
        up = jnp.dot(hidden_two, w_up, preferred_element_type=jnp.float32)
        act = (jax.nn.silu(gate) * up).astype(jnp.bfloat16)
        result = mid + jnp.dot(act, w_down, preferred_element_type=jnp.float32)
        outputs.append(result.astype(jnp.bfloat16)[positions])
        down_term = outer_sum(act, grad_out)
        act_grad = jnp.dot(grad_out, w_down.T, preferred_element_type=jnp.float32)
        sigmoid_gate = jax.nn.sigmoid(gate)
        gate_grad = (act_grad * up * sigmoid_gate * (1.0 + gate * (1.0 - sigmoid_gate))).astype(jnp.bfloat16)
        up_grad = (act_grad * jax.nn.silu(gate)).astype(jnp.bfloat16)
        gate_term = outer_sum(hidden_two, gate_grad)
        up_term = outer_sum(hidden_two, up_grad)
        hidden_two_grad = jnp.dot(gate_grad, w_gate.T, preferred_element_type=jnp.float32) + jnp.dot(up_grad, w_up.T, preferred_element_type=jnp.float32)
        gain_two_term = lax.optimization_barrier(jnp.sum(hidden_two_grad * normed_two, axis=0))
        weighted = hidden_two_grad * gain_two
        mid_grad = grad_out.astype(jnp.float32) + scale_two * (weighted - normed_two * lax.optimization_barrier(jnp.mean(weighted * normed_two, axis=-1, keepdims=True)))
        proj_grad = mid_grad.astype(jnp.bfloat16)
        out_term = outer_sum(attended, proj_grad)
        attended_grad = jnp.dot(proj_grad, w_out.T, preferred_element_type=jnp.float32).astype(jnp.bfloat16)
        query_grad, key_grad, value_grad = attend_backward(queries, keys, values.reshape(SEQLEN, KVH, HD), attended, attended_grad, log_total, query_block)
        query_back = rotate(query_grad.reshape(SEQLEN, H, HD), cosines, -sines).astype(jnp.bfloat16).reshape(SEQLEN, H * HD)
        key_back = rotate(key_grad, cosines, -sines).astype(jnp.bfloat16).reshape(SEQLEN, KVH * HD)
        value_back = value_grad.astype(jnp.bfloat16).reshape(SEQLEN, KVH * HD)
        query_term = outer_sum(hidden_one, query_back)
        key_term = outer_sum(hidden_one, key_back)
        value_term = outer_sum(hidden_one, value_back)
        hidden_one_grad = jnp.dot(query_back, w_query.T, preferred_element_type=jnp.float32) + jnp.dot(key_back, w_key.T, preferred_element_type=jnp.float32) + jnp.dot(value_back, w_value.T, preferred_element_type=jnp.float32)
        gain_one_term = lax.optimization_barrier(jnp.sum(hidden_one_grad * normed_one, axis=0))
        weighted_one = hidden_one_grad * gain_one
        grad_in = mid_grad + scale_one * (weighted_one - normed_one * lax.optimization_barrier(jnp.mean(weighted_one * normed_one, axis=-1, keepdims=True)))
        input_grads.append(grad_in.astype(jnp.bfloat16)[positions])
        terms = (gain_one_term, gain_two_term, query_term, key_term, value_term, out_term, gate_term, up_term, down_term)
        totals = terms if totals is None else tuple((a + b for a, b in zip(totals, terms)))
    return (jnp.stack(outputs), jnp.stack(input_grads), totals[0], totals[1], totals[2], totals[3], totals[4], totals[5], totals[6], totals[7], totals[8])
```

```python
import jax
import jax.numpy as jnp
from jax import lax
from jax.experimental import pallas as pl
from jax.experimental.pallas import tpu as pltpu
from jax.sharding import PartitionSpec as P

H = 9
KVH = 3
HD = 64
GROUP = H // KVH
EPS = 1e-05
THETA = 100000.0
NEGATIVE = -1e30
bf16 = jnp.bfloat16
f32 = jnp.float32


def nn(a, b):
    return lax.dot_general(a, b, (((1,), (0,)), ((), ())), preferred_element_type=f32)


def nt(a, b):
    return lax.dot_general(a, b, (((1,), (1,)), ((), ())), preferred_element_type=f32)


def tn(a, b):
    return lax.dot_general(a, b, (((0,), (0,)), ((), ())), preferred_element_type=f32)


def rms_scale(rows):
    return lax.rsqrt(jnp.mean(rows * rows, axis=-1, keepdims=True) + EPS)


def shape(*dims, dtype=bf16):
    return jax.ShapeDtypeStruct(dims, dtype)


def call(kernel, outs, scalars, *args, scratch=(), name=None):
    return pl.pallas_call(
        kernel,
        out_shape=tuple(outs),
        in_specs=[pl.BlockSpec(memory_space=pltpu.SMEM)]
        + [pl.BlockSpec(memory_space=pltpu.VMEM) for _ in args],
        out_specs=tuple(pl.BlockSpec(memory_space=pltpu.VMEM) for _ in outs),
        scratch_shapes=list(scratch),
        compiler_params=pltpu.CompilerParams(vmem_limit_bytes=60 * 2**20),
        name=name,
    )(scalars, *args)


def over(x, axis, k):
    n = lax.axis_size(axis)
    return lax.ppermute(x, axis, [(i, i ^ k) for i in range(n)])


def gather_plane(x):
    mine = [x] + [over(x, "ctx", k) for k in range(1, lax.axis_size("ctx"))]
    return mine + [over(piece, "seq", 1) for piece in mine]


def turned_lanes(u):
    width = u.shape[1]
    lane = lax.broadcasted_iota(jnp.int32, u.shape, 1) & (HD - 1)
    half = HD // 2
    return jnp.where(lane < half, -pltpu.roll(u, width - half, 1), pltpu.roll(u, half, 1))


def qkv_kernel(
    sc, x_ref, own_ref, other_ref, cos_ref, sin_ref,
    h_ref, q_ref, kv_ref, wq_ref, wkv_ref, wo_ref, gain_ref,
):
    rows, dim = x_ref.shape
    width = KVH * HD

    def compute(a_ref, b_ref):
        gains = a_ref[:, dim + width :].astype(f32).T
        gain_ref[...] = gains[:8]
        x = x_ref[...].astype(f32)
        hidden = (x * rms_scale(x) * gains[0:1]).astype(bf16)
        h_ref[...] = hidden
        first = nn(hidden, a_ref[...])[:, : dim + width]
        values = nn(hidden, b_ref[:, : width + HD])[:, :width]
        times = (dim + width) // (2 * HD)
        cosines = jnp.concatenate([cos_ref[...]] * times, axis=1)
        sines = jnp.concatenate([sin_ref[...]] * times, axis=1)
        turned = (first * cosines + turned_lanes(first) * sines).astype(bf16)
        for head in range(H):
            q_ref[head * rows : (head + 1) * rows, :] = (
                turned[:, head * HD : (head + 1) * HD] * HD ** (-0.5)
            ).astype(bf16)
        kv_ref[...] = jnp.concatenate([turned[:, dim:], values.astype(bf16)], axis=1)
        wq_ref[...] = a_ref[:, :dim]
        wkv_ref[...] = jnp.concatenate([a_ref[:, dim : dim + width], b_ref[:, :width]], axis=1)
        wo_ref[...] = b_ref[:, width + HD :]

    @pl.when(sc[0] == 0)
    def _():
        compute(own_ref, other_ref)

    @pl.when(sc[0] != 0)
    def _():
        compute(other_ref, own_ref)


def places(sc, rows, block):
    c, z = sc[1], sc[2]
    start = z * rows
    mine = sc[3 + 2 * c + lax.div(start, block)]
    return mine, lax.rem(start, block)


def allowed_pairs(block, wide, rows, place, mine, offset):
    key = place * block + lax.broadcasted_iota(jnp.int32, (block, wide), 0)
    lane = lax.broadcasted_iota(jnp.int32, (block, wide), 1)
    return key <= mine * block + offset + lax.rem(lane, rows)


def forward_kernel(*refs, count):
    sc, x_ref, q_ref, wo_ref, gain_ref = refs[:5]
    pieces = refs[5 : 5 + count]
    all_ref, att_ref, log_ref, mid_ref, h_ref, top_s, tot_s, acc_s = refs[5 + count :]
    rows = x_ref.shape[0]
    span = pieces[0].shape[0]
    block = span // 2
    wide = GROUP * rows
    width = KVH * HD
    for k in range(count):
        all_ref[k * span : (k + 1) * span, :] = pieces[k][...]
    mine, offset = places(sc, rows, block)
    top_s[...] = jnp.full(top_s.shape, NEGATIVE, f32)
    tot_s[...] = jnp.zeros(tot_s.shape, f32)
    acc_s[...] = jnp.zeros(acc_s.shape, f32)

    def step(t, carry):
        place = sc[3 + 2 * (sc[1] ^ lax.shift_right_logical(t, 1)) + (t & 1)]

        @pl.when(place <= mine)
        def _():
            part = all_ref[pl.ds(pl.multiple_of(t * block, block), block), :]
            ok = allowed_pairs(block, wide, rows, place, mine, offset)
            for g in range(KVH):
                keys = part[:, g * HD : (g + 1) * HD]
                values = part[:, width + g * HD : width + (g + 1) * HD]
                scores = jnp.where(ok, nt(keys, q_ref[g * wide : (g + 1) * wide, :]), NEGATIVE)
                old = top_s[g]
                top = jnp.maximum(old, jnp.max(scores, axis=0, keepdims=True))
                weights = jnp.where(ok, jnp.exp(scores - top), 0.0)
                factor = jnp.exp(old - top)
                tot_s[g] = factor * tot_s[g] + jnp.sum(weights, axis=0, keepdims=True)
                acc_s[g] = factor * acc_s[g] + tn(values, weights.astype(bf16))
                top_s[g] = top

        return carry

    lax.fori_loop(0, 2 * count, step, 0)
    heads = []
    for g in range(KVH):
        out = acc_s[g] / tot_s[g]
        log_ref[g] = top_s[g] + jnp.log(tot_s[g])
        for h in range(GROUP):
            heads.append(out[:, h * rows : (h + 1) * rows])
    attended = jnp.concatenate(heads, axis=0).T.astype(bf16)
    att_ref[...] = attended
    mid = x_ref[...].astype(f32) + nt(attended, wo_ref[...])
    mid_ref[...] = mid
    h_ref[...] = (mid * rms_scale(mid) * gain_ref[1:2, :]).astype(bf16)


def mlp_kernel(*refs, plane, zs):
    sc, w_ref = refs[:2]
    hs = refs[2 : 2 + plane]
    cots = refs[2 + plane : 2 + 2 * plane]
    rest = refs[2 + 2 * plane :]
    back_keep, back_send, out_keep, out_send = rest[:4]
    grads = rest[4 : 4 + zs]
    h_s, c_s, act_s, gg_s, ug_s, dw_s = rest[4 + zs :]
    rows, dim = hs[0].shape
    cut = w_ref.shape[1] // 3
    for k in range(plane):
        h_s[k * rows : (k + 1) * rows, :] = hs[k][...]
        c_s[k * rows : (k + 1) * rows, :] = cots[k][...]
    w_pair = w_ref[:, : 2 * cut]
    w_gate = w_ref[:, :cut]
    w_up = w_ref[:, cut : 2 * cut]
    w_down = w_ref[:, 2 * cut :]
    total = plane * rows
    half = total // 2
    chunk = min(2 * rows, half)
    for start in range(0, total, chunk):
        here = slice(start, start + chunk)
        both = nn(h_s[here, :], w_pair)
        gate = both[:, :cut]
        up = both[:, cut:]
        act_grad = nn(c_s[here, :], w_down)
        sig = jax.nn.sigmoid(gate)
        silu = gate * sig
        act = (silu * up).astype(bf16)
        gate_grad = (act_grad * up * sig * (1.0 + gate * (1.0 - sig))).astype(bf16)
        up_grad = (act_grad * silu).astype(bf16)
        act_s[here, :] = act
        gg_s[here, :] = gate_grad
        ug_s[here, :] = up_grad
        back = (nt(gate_grad, w_gate) + nt(up_grad, w_up)).astype(bf16)
        out = nt(act, w_down).astype(bf16)
        if start < half:
            back_keep[here, :] = back
            out_keep[here, :] = out
        else:
            there = slice(start - half, start - half + chunk)
            back_send[there, :] = back
            out_send[there, :] = out
    dw_s[:, :cut] = tn(h_s[...], gg_s[...])
    dw_s[:, cut : 2 * cut] = tn(h_s[...], ug_s[...])
    dw_s[:, 2 * cut :] = tn(c_s[...], act_s[...])
    deep = dim // zs
    for k in range(zs):
        start = pl.multiple_of((sc[2] ^ k) * deep, 8)
        grads[k][...] = dw_s[pl.ds(start, deep), :].astype(bf16)


def pair_kernel(sc, keep_ref, got_ref, *outs):
    rows = outs[0].shape[0]
    for k, out in enumerate(outs):
        here = slice(k * rows, (k + 1) * rows)
        out[...] = (keep_ref[here, :].astype(f32) + got_ref[here, :].astype(f32)).astype(out.dtype)


def backward_kernel(*refs, count):
    sc, mid_ref, cot_ref, gain_ref, wo_ref, att_ref, log_ref, q_ref, all_ref = refs[:9]
    sums = refs[9 : 9 + count]
    midg_ref, pg_ref, g2_ref, dq_ref = refs[9 + count : 13 + count]
    outs = refs[13 + count : 13 + 2 * count]
    do_s, delta_s, dkv_s = refs[13 + 2 * count :]
    rows, dim = mid_ref.shape
    span = outs[0].shape[0]
    block = span // 2
    wide = GROUP * rows
    width = KVH * HD
    back = sums[0][...].astype(f32)
    for piece in sums[1:]:
        back = back + piece[...].astype(f32)
    mid = mid_ref[...]
    scale = rms_scale(mid)
    normed = mid * scale
    g2_ref[...] = jnp.broadcast_to(jnp.sum(back * normed, axis=0, keepdims=True), g2_ref.shape)
    weighted = back * gain_ref[1:2, :]
    mid_grad = cot_ref[...].astype(f32) + scale * (
        weighted - normed * jnp.mean(weighted * normed, axis=-1, keepdims=True)
    )
    midg_ref[...] = mid_grad
    proj = mid_grad.astype(bf16)
    pg_ref[...] = proj
    attg = nn(proj, wo_ref[...]).astype(bf16)
    product = (attg.astype(f32) * att_ref[...].astype(f32)).T
    for head in range(H):
        g, h = divmod(head, GROUP)
        do_s[head * rows : (head + 1) * rows, :] = attg[:, head * HD : (head + 1) * HD]
        delta_s[g, :, h * rows : (h + 1) * rows] = jnp.sum(
            product[head * HD : (head + 1) * HD, :], axis=0, keepdims=True
        )
    dq_ref[...] = jnp.zeros(dq_ref.shape, f32)
    mine, offset = places(sc, rows, block)

    def step(t, carry):
        place = sc[3 + 2 * (sc[1] ^ lax.shift_right_logical(t, 1)) + (t & 1)]
        here = pl.ds(pl.multiple_of(t * block, block), block)

        @pl.when(place > mine)
        def _():
            dkv_s[here, :] = jnp.zeros((block, 2 * width), bf16)

        @pl.when(place <= mine)
        def _():
            part = all_ref[here, :]
            ok = allowed_pairs(block, wide, rows, place, mine, offset)
            key_parts = []
            value_parts = []
            for g in range(KVH):
                keys = part[:, g * HD : (g + 1) * HD]
                values = part[:, width + g * HD : width + (g + 1) * HD]
                queries = q_ref[g * wide : (g + 1) * wide, :]
                grads = do_s[g * wide : (g + 1) * wide, :]
                scores = nt(keys, queries)
                probs = jnp.where(ok, jnp.exp(jnp.where(ok, scores, NEGATIVE) - log_ref[g]), 0.0)
                score_grad = (probs * (nt(values, grads) - delta_s[g])).astype(bf16)
                value_parts.append(nn(probs.astype(bf16), grads))
                key_parts.append(nn(score_grad, queries))
                dq_ref[g * HD : (g + 1) * HD, :] += tn(keys, score_grad)
            dkv_s[here, :] = jnp.concatenate(key_parts + value_parts, axis=1).astype(bf16)

        return carry

    lax.fori_loop(0, 2 * count, step, 0)
    for k in range(count):
        outs[k][...] = dkv_s[k * span : (k + 1) * span, :]


def query_kernel(
    sc, dq_ref, cost_ref, sint_ref, h_ref, pg_ref, att_ref, wq_ref, g2_ref,
    hq_ref, keep_ref, send_ref, both_s,
):
    rows, dim = h_ref.shape
    half = HD // 2
    heads = []
    for head in range(H):
        g, h = divmod(head, GROUP)
        u = dq_ref[g * HD : (g + 1) * HD, h * rows : (h + 1) * rows] * HD ** (-0.5)
        turned = jnp.concatenate([-u[half:], u[:half]], axis=0)
        heads.append(u * cost_ref[...] - turned * sint_ref[...])
    back = jnp.concatenate(heads, axis=0).T.astype(bf16)
    hq_ref[...] = nt(back, wq_ref[...])
    both_s[0, :, :dim] = tn(h_ref[...], back)
    both_s[0, :, dim:] = jnp.broadcast_to(g2_ref[0:1, :], (HD, dim)).T
    both_s[1, :, :dim] = tn(pg_ref[...], att_ref[...])
    both_s[1, :, dim:] = jnp.zeros((dim, HD), f32)
    keep_ref[...] = both_s[sc[0]].astype(bf16)
    send_ref[...] = both_s[1 - sc[0]].astype(bf16)


def split_kernel(sc, *refs, parts, rowsplit):
    ins = refs[:parts]
    outs = refs[parts:-1]
    total = ins[0][...].astype(f32)
    for piece in ins[1:]:
        total = total + piece[...].astype(f32)
    sum_s = refs[-1]
    sum_s[...] = total
    for k, out in enumerate(outs):
        start = pl.multiple_of((sc[2] ^ k) * rowsplit, 8)
        out[...] = sum_s[pl.ds(start, rowsplit), :].astype(out.dtype)


def last_kernel(*refs, zs):
    sc, x_ref, midg_ref, hq_ref, h_ref, wkv_ref, gain_ref, cos_ref, sin_ref = refs[:9]
    pieces = refs[9 : 9 + zs]
    gin_ref, keep_ref, send_ref, both_s = refs[9 + zs :]
    dim = x_ref.shape[1]
    width = KVH * HD
    total = pieces[0][...].astype(f32)
    for piece in pieces[1:]:
        total = total + piece[...].astype(f32)
    times = width // HD
    cosines = jnp.concatenate([cos_ref[...]] * times, axis=1)
    sines = jnp.concatenate([sin_ref[...]] * times, axis=1)
    lane = lax.broadcasted_iota(jnp.int32, total.shape, 1)
    back = jnp.where(
        lane < width, total * cosines - turned_lanes(total) * sines, total
    ).astype(bf16)
    hidden_grad = hq_ref[...] + nt(back, wkv_ref[...])
    x = x_ref[...].astype(f32)
    scale = rms_scale(x)
    normed = x * scale
    gain_term = jnp.sum(hidden_grad * normed, axis=0, keepdims=True)
    weighted = hidden_grad * gain_ref[0:1, :]
    gin_ref[...] = (
        midg_ref[...]
        + scale * (weighted - normed * jnp.mean(weighted * normed, axis=-1, keepdims=True))
    ).astype(bf16)
    grads = tn(h_ref[...], back)
    both_s[0, :, :width] = grads[:, :width]
    both_s[0, :, width:] = jnp.broadcast_to(gain_term, (HD, dim)).T
    both_s[1, :, :width] = grads[:, width:]
    both_s[1, :, width:] = jnp.zeros((dim, HD), f32)
    keep_ref[...] = both_s[sc[0]].astype(bf16)
    send_ref[...] = both_s[1 - sc[0]].astype(bf16)


def place_kernel(*refs, plane):
    sc = refs[0]
    pieces = refs[1 : 1 + plane]
    gate_ref, up_ref, down_ref, gate_s, up_s = refs[1 + plane :]
    count = plane // 2
    cut = pieces[0].shape[1] // 3
    for k in range(plane):
        rank = (sc[0] ^ (k // count)) * count + (sc[1] ^ (k % count))
        piece = pieces[k][...].astype(f32)
        gate_s[rank] = piece[:, :cut]
        up_s[rank] = piece[:, cut : 2 * cut]
        down_ref[pl.ds(pl.multiple_of(rank * cut, 8), cut), :] = piece[:, 2 * cut :].T
    for k in range(plane):
        gate_ref[:, k * cut : (k + 1) * cut] = gate_s[k]
        up_ref[:, k * cut : (k + 1) * cut] = up_s[k]


def body(
    tokens, block_order, attn_gain, mlp_gain, w_query, w_key, w_value, w_out, w_gate, w_up,
    w_down, cotangent,
):
    s = lax.axis_index("seq")
    c = lax.axis_index("ctx")
    z = lax.axis_index("fsdp")
    count = lax.axis_size("ctx")
    zs = lax.axis_size("fsdp")
    plane = count * lax.axis_size("seq")
    x = tokens[0]
    cot = cotangent[0]
    rows, dim = x.shape
    deep = w_query.shape[0]
    ff = w_gate.shape[1]
    cut = ff // plane
    width = KVH * HD
    span = rows * zs
    block = span // 2
    wide = GROUP * rows
    scalars = jnp.concatenate(
        [jnp.stack([s, c, z]).astype(jnp.int32), block_order[0].astype(jnp.int32)]
    )

    first = jnp.concatenate(
        [w_query, w_key, attn_gain[:, None], mlp_gain[:, None], jnp.zeros((deep, HD - 2), bf16)],
        axis=1,
    )
    second = jnp.concatenate([w_value, jnp.zeros((deep, HD), bf16), w_out.T], axis=1)
    cots = gather_plane(cot)
    own_half = lax.all_gather(jnp.where(s == 0, first, second), "fsdp", axis=0, tiled=True)
    other_half = over(own_half, "seq", 1)

    which = 2 * c + (z * rows) // block
    mine = jnp.sum(jnp.where(jnp.arange(block_order.shape[1]) == which, block_order[0], 0))
    base = mine * block + (z * rows) % block
    pos = (base + jnp.arange(rows, dtype=jnp.int32)).astype(f32)
    inverse = jnp.power(THETA, -jnp.arange(HD // 2, dtype=f32) * 2.0 / HD)
    angles = pos[:, None] * jnp.concatenate([inverse] * 4)[None, :]
    cosines, sines = jnp.cos(angles), jnp.sin(angles)
    cosines_t, sines_t = cosines[:, :HD].T, sines[:, :HD].T

    hidden, q, kv, wq, wkv, wo, gains = call(
        qkv_kernel,
        [
            shape(rows, dim), shape(H * rows, HD), shape(rows, 2 * width), shape(dim, dim),
            shape(dim, 2 * width), shape(dim, dim), shape(8, dim, dtype=f32),
        ],
        scalars, x, own_half, other_half, cosines, sines, name="qkv",
    )
    kv_z = lax.all_gather(kv, "fsdp", axis=0, tiled=True)
    pieces = [kv_z] + [over(kv_z, "ctx", k) for k in range(1, count)]

    rank = s * count + c
    cut_pack = jnp.concatenate(
        [
            lax.dynamic_slice(w_gate, (0, rank * cut), (deep, cut)),
            lax.dynamic_slice(w_up, (0, rank * cut), (deep, cut)),
            lax.dynamic_slice(w_down, (rank * cut, 0), (cut, deep)).T,
        ],
        axis=1,
    )
    cut_pack, kv_z2 = lax.optimization_barrier((cut_pack, kv_z))
    w_mlp = lax.all_gather(cut_pack, "fsdp", axis=0, tiled=True)

    kv_all, attended, log_total, mid, hidden2 = call(
        lambda *refs: forward_kernel(*refs, count=count),
        [
            shape(span * count, 2 * width), shape(rows, dim), shape(KVH, 1, wide, dtype=f32),
            shape(rows, dim, dtype=f32), shape(rows, dim),
        ],
        scalars, x, q, wo, gains, *pieces,
        scratch=[
            pltpu.VMEM((KVH, 1, wide), f32), pltpu.VMEM((KVH, 1, wide), f32),
            pltpu.VMEM((KVH, HD, wide), f32),
        ],
        name="forward",
    )
    hs = gather_plane(hidden2)
    outs = call(
        lambda *refs: mlp_kernel(*refs, plane=plane, zs=zs),
        [shape(count * rows, dim)] * 4 + [shape(deep, 3 * cut)] * zs,
        scalars, w_mlp, *hs, *cots,
        scratch=[
            pltpu.VMEM((plane * rows, dim), bf16), pltpu.VMEM((plane * rows, dim), bf16),
            pltpu.VMEM((plane * rows, cut), bf16), pltpu.VMEM((plane * rows, cut), bf16),
            pltpu.VMEM((plane * rows, cut), bf16), pltpu.VMEM((dim, 3 * cut), f32),
        ],
        name="mlp",
    )
    back_keep, back_send, out_keep, out_send = outs[:4]
    mlp_grads = outs[4:]
    back_got = over(back_send, "seq", 1)
    sums = call(
        pair_kernel, [shape(rows, dim, dtype=f32)] + [shape(rows, dim)] * (count - 1),
        scalars, back_keep, back_got, name="back_pair",
    )
    sums = [sums[0]] + [over(sums[k], "ctx", k) for k in range(1, count)]
    mid_grad, proj, gain2_term, dq, *dkv = call(
        lambda *refs: backward_kernel(*refs, count=count),
        [
            shape(rows, dim, dtype=f32), shape(rows, dim), shape(8, dim, dtype=f32),
            shape(KVH * HD, wide, dtype=f32),
        ]
        + [shape(span, 2 * width)] * count,
        scalars, mid, cot, gains, wo, attended, log_total, q, kv_all, *sums,
        scratch=[
            pltpu.VMEM((H * rows, HD), bf16), pltpu.VMEM((KVH, 1, wide), f32),
            pltpu.VMEM((span * count, 2 * width), bf16),
        ],
        name="backward",
    )
    dkv = [dkv[0]] + [over(dkv[k], "ctx", k) for k in range(1, count)]

    out_got = over(out_send, "seq", 1)
    out_sums = call(
        pair_kernel, [shape(rows, dim, dtype=f32)] + [shape(rows, dim)] * (count - 1),
        scalars, out_keep, out_got, name="out_pair",
    )
    out_sums = [out_sums[0]] + [over(out_sums[k], "ctx", k) for k in range(1, count)]
    layer_out = (mid + sum(piece.astype(f32) for piece in out_sums)).astype(bf16)

    def along_z(chunks):
        got = [chunks[0]] + [over(chunks[k], "fsdp", k) for k in range(1, zs)]
        return sum(piece.astype(f32) for piece in got)

    def across(part):
        part = part.astype(bf16)
        total = sum(
            piece.astype(f32)
            for piece in [part] + [over(part, "ctx", k) for k in range(1, count)]
        ).astype(bf16)
        other = over(total, "seq", 1)
        return (
            jnp.where(s == 0, total, other).astype(f32),
            jnp.where(s == 0, other, total).astype(f32),
        )

    def reduce_halves(keep, send):
        got = over(send, "seq", 1)
        chunks = call(
            lambda *refs: split_kernel(*refs, parts=2, rowsplit=deep),
            [shape(deep, keep.shape[1])] * zs,
            scalars, keep, got, scratch=[pltpu.VMEM(keep.shape, f32)], name="halves",
        )
        return across(along_z(chunks))

    mlp_part = gather_plane(along_z(mlp_grads).astype(bf16))
    hq, keep_a, send_a = call(
        query_kernel,
        [shape(rows, dim, dtype=f32)] + [shape(dim, dim + HD)] * 2,
        scalars, dq, cosines_t, sines_t, hidden, proj, attended, wq, gain2_term,
        scratch=[pltpu.VMEM((2, dim, dim + HD), f32)], name="query",
    )
    d_query, d_out = reduce_halves(keep_a, send_a)
    d_gate, d_up, d_down = call(
        lambda *refs: place_kernel(*refs, plane=plane),
        [shape(deep, ff, dtype=f32), shape(deep, ff, dtype=f32), shape(ff, deep, dtype=f32)],
        scalars, *mlp_part,
        scratch=[pltpu.VMEM((plane, deep, cut), f32), pltpu.VMEM((plane, deep, cut), f32)],
        name="place",
    )

    dkv_chunks = call(
        lambda *refs: split_kernel(*refs, parts=count, rowsplit=rows),
        [shape(rows, 2 * width)] * zs,
        scalars, *dkv, scratch=[pltpu.VMEM((span, 2 * width), f32)], name="dkv_sum",
    )
    dkv_own = [dkv_chunks[0]] + [over(dkv_chunks[k], "fsdp", k) for k in range(1, zs)]
    grad_in, keep_b, send_b = call(
        lambda *refs: last_kernel(*refs, zs=zs),
        [shape(rows, dim), shape(dim, width + HD), shape(dim, width + HD)],
        scalars, x, mid_grad, hq, hidden, wkv, gains, cosines, sines, *dkv_own,
        scratch=[pltpu.VMEM((2, dim, width + HD), f32)], name="last",
    )
    d_key, d_value = reduce_halves(keep_b, send_b)
    return (
        layer_out[None],
        grad_in[None],
        d_key[:, width],
        d_query[:, dim],
        d_query[:, :dim],
        d_key[:, :width],
        d_value[:, :width],
        d_out[:, :dim].T,
        d_gate,
        d_up,
        d_down,
    )


def solution(mesh):
    rows = P("seq", ("ctx", "fsdp"), None)
    first = P("fsdp", None)
    second = P(None, "fsdp")
    return jax.shard_map(
        body,
        mesh=mesh,
        in_specs=(
            rows, P("seq", None), P("fsdp"), P("fsdp"), first, first, first, second, first,
            first, second, rows,
        ),
        out_specs=(
            rows, rows, P("fsdp"), P("fsdp"), first, first, first, second, first, first, second,
        ),
        check_vma=False,
    )
```
